128 devices in a mesh: row: 4 (over x), col: 16 (over z, y), depth: 2 (over core).
Axes of the slice: x: 4, y: 4, z: 4, core: 2. Of those that a mesh axis runs over, the one named last changes fastest.
Arguments:
- tokens: bfloat16 [2048, 8192], P('depth', 'col'), may hold values from -6 to 6
- weight: bfloat16 [8192, 14336], P('col', ('row', 'depth')), may hold values from -0.0625 to 0.0625
- block_mask: int32 [64, 112], replicated, may hold values 0 or 1
- cotangent: bfloat16 [2048, 14336], P('depth', 'row'), may hold values from -6 to 6
- example_ids: int32 [2048], replicated, may hold values from 0 to 3, as said below
Outputs:
- outputs: bfloat16 [2048, 14336], P('depth', 'row')
- grad_in: bfloat16 [2048, 8192], P('depth', 'col')
- grad_weight: bfloat16 [8192, 14336], P('col', ('row', 'depth'))
The draws below stay inside these ranges and needn't reach their ends.
Inputs may be any that keep to these rules, and one draw needn't show every extreme that they name: `example_ids`: in the b-th aligned block of 1024 tokens (b from 0), the ids are 2 b for a first run of tokens and 2 b + 1 for the rest; each example has at least 128 tokens, and in every draw some example has exactly 896.
All inputs are finite; a program needn't handle non-finite values.
Results may differ from the reference program's by a relative error of at most 0.0052.
Values may be sent and summed in bfloat16 or wider, within the bound.
A program may use at most 128 MiB of HBM per device.

```python
import jax
import jax.numpy as jnp
from jax import lax

D = 8192
FW = 14336
BLOCK = 128
TOK_DEV = 1024
EX_DEV = 2
TOKENS = 2048
EXAMPLES = 4
N_DEPTH = 2


def draw_example_ids(key, part):
    blocks = TOKENS // TOK_DEV
    shortest = TOK_DEV // 8
    first_key, second_key = jax.random.split(jax.random.fold_in(key, 17))
    cuts = jax.random.randint(first_key, (blocks,), shortest, TOK_DEV - shortest + 1)
    chosen = jax.random.randint(second_key, (), 0, blocks)
    cuts = jnp.where(jnp.arange(blocks) == chosen, shortest, cuts)
    places = jnp.arange(TOK_DEV)
    later = (places[None, :] >= cuts[:, None]).astype(jnp.int32)
    ids = 2 * jnp.arange(blocks, dtype=jnp.int32)[:, None] + later
    return ids.reshape(-1).astype(jnp.int32)


def plant(result, stream_key, low, high):
    spot = [jax.random.randint(jax.random.fold_in(stream_key, axis), (), 0, length) for axis, length in enumerate(result.shape)]
    longest = result.shape.index(max(result.shape))
    beside = spot[:longest] + [(spot[longest] + 1) % result.shape[longest]] + spot[longest + 1:]
    return result.at[tuple(spot)].set(low).at[tuple(beside)].set(high)


def steps_of(rng, dims, cuts, least, largest):
    gain = 1.0
    for dim, blocks in cuts:
        draws = jax.random.uniform(jax.random.fold_in(jax.random.fold_in(rng, 6), dim), (blocks,), jnp.float32, least / len(cuts), largest / len(cuts))
        gain = gain * jnp.repeat(jnp.exp(draws), dims[dim] // blocks).reshape((-1,) + (1,) * (len(dims) - 1 - dim))
    return gain


def normal_values(stream_key, dims, deviation, limit, cuts=(), kind=jnp.bfloat16):
    drawn = deviation * jax.random.normal(stream_key, dims, jnp.float32)
    if cuts:
        drawn = drawn * steps_of(stream_key, dims, cuts, -0.22, 0.18)
    return jnp.clip(drawn, -limit, limit).astype(kind)


def setup_inputs(seed: int = 0) -> dict:
    arg_keys = jax.random.split(jax.random.key(seed), 6)
    return {
        "tokens": normal_values(arg_keys[0], (TOKENS, D), 1.0, 6.0, ((0, 2), (1, 16))),
        "weight": normal_values(arg_keys[1], (D, FW), D ** -0.5, 0.0625, ((0, 16), (1, 8))),
        "block_mask": plant((jax.random.randint(arg_keys[2], (D // BLOCK, FW // BLOCK), 0, 2) < 1).astype(jnp.int32), jax.random.fold_in(arg_keys[2], 1), 0, 1),
        "cotangent": normal_values(arg_keys[3], (TOKENS, FW), 1.0, 6.0, ((0, 2), (1, 4))),
        "example_ids": draw_example_ids(jax.random.fold_in(arg_keys[5], 71), 0),
    }


def reference(tokens, weight, block_mask, cotangent, example_ids):
    keep = jnp.repeat(jnp.repeat(block_mask > 0, BLOCK, axis=0), BLOCK, axis=1)
    masked = jnp.where(keep, weight, jnp.zeros((), jnp.bfloat16))
    outputs = jnp.dot(tokens, masked, preferred_element_type=jnp.float32).astype(jnp.bfloat16)
    grad_in = jnp.dot(cotangent, masked.T, preferred_element_type=jnp.float32).astype(jnp.bfloat16)
    bound = 0.5 * jnp.sqrt(jnp.float32(D) * jnp.float32(FW) * jnp.float32(TOK_DEV))
    total = jnp.zeros((D, FW), jnp.float32)
    for block_at in range(N_DEPTH):
        rows_x = tokens[block_at * TOK_DEV:(block_at + 1) * TOK_DEV]
        rows_g = cotangent[block_at * TOK_DEV:(block_at + 1) * TOK_DEV]
        rows_id = example_ids[block_at * TOK_DEV:(block_at + 1) * TOK_DEV]
        terms = jnp.zeros((D, FW), jnp.float32)
        for slot in range(EX_DEV):
            chosen = rows_id == block_at * EX_DEV + slot
            picked = jnp.where(chosen[:, None], rows_g, jnp.zeros((), jnp.bfloat16))
            product = lax.dot_general(rows_x, picked, (((0,), (0,)), ((), ())), preferred_element_type=jnp.float32)
            product = jnp.where(keep, product, jnp.float32(0.0))
            norm_value = jnp.sqrt(jnp.sum(product * product))
            terms = terms + bound / jnp.maximum(norm_value, bound) * product
        rounded = lax.optimization_barrier((terms / EXAMPLES).astype(jnp.bfloat16))
        total = total + rounded.astype(jnp.float32)
    grad_weight = total.astype(jnp.bfloat16)
    return (outputs, grad_in, grad_weight)
```

```python
import math

import jax
import jax.numpy as jnp
from jax import lax
from jax.sharding import PartitionSpec as P

D = 8192
FW = 14336
BLOCK = 128
TOK_DEV = 1024
EX_DEV = 2


def total_squares(partial_squares):
    return lax.psum(partial_squares, ("row", "col"))


def shards(tokens, weight, block_mask, cotangent, example_ids):
    tok_rows = tokens.shape[0]
    width_here = tokens.shape[1]
    hidden_here = cotangent.shape[1]
    col_at = lax.axis_index("col")
    row_at = lax.axis_index("row")
    depth_at = lax.axis_index("depth")
    tile_mask = lax.dynamic_slice(
        block_mask,
        (col_at * (width_here // BLOCK), row_at * (hidden_here // BLOCK)),
        (width_here // BLOCK, hidden_here // BLOCK),
    )
    keep = jnp.repeat(jnp.repeat(tile_mask > 0, BLOCK, axis=0), BLOCK, axis=1)
    zero_half = jnp.zeros((), jnp.bfloat16)
    ids_here = lax.dynamic_slice_in_dim(example_ids, depth_at * tok_rows, tok_rows)
    per_grads = []
    squares = []
    for slot in range(EX_DEV):
        chosen = ids_here == depth_at * EX_DEV + slot
        picked = jnp.where(chosen[:, None], cotangent, zero_half)
        product = lax.dot_general(
            tokens, picked, (((0,), (0,)), ((), ())), preferred_element_type=jnp.float32
        )
        product = jnp.where(keep, product, jnp.float32(0.0))
        per_grads.append(product)
        squares.append(jnp.sum(product * product))
    partial_squares = jnp.stack(squares)
    kept = keep
    out_part = jnp.dot(
        tokens,
        jnp.where(kept, lax.all_gather(weight, "depth", axis=1, tiled=True), zero_half),
        preferred_element_type=jnp.float32,
    )
    kept = keep
    masked_piece = jnp.where(kept, lax.all_gather(weight, "depth", axis=1, tiled=True), zero_half)
    back_part = lax.dot_general(
        cotangent, masked_piece, (((1,), (1,)), ((), ())), preferred_element_type=jnp.float32
    )
    out_sum = lax.all_gather(
        lax.psum_scatter(out_part.astype(jnp.bfloat16), "col", scatter_dimension=0, tiled=True), "col", axis=0, tiled=True
    )
    back_sum = lax.all_gather(
        lax.psum_scatter(back_part.astype(jnp.bfloat16), "row", scatter_dimension=0, tiled=True), "row", axis=0, tiled=True
    )
    all_squares = total_squares(partial_squares)
    out_final = out_sum.astype(jnp.bfloat16)
    back_final = back_sum.astype(jnp.bfloat16)
    bound = jnp.float32(0.5 * math.sqrt(D * FW * TOK_DEV))
    norms = jnp.sqrt(all_squares)
    factors = bound / jnp.maximum(norms, bound)
    examples_all = EX_DEV * lax.axis_size("depth")
    combined = jnp.zeros((width_here, hidden_here), jnp.float32)
    for slot in range(EX_DEV):
        combined = combined + factors[slot] * per_grads[slot]
    combined = combined / examples_all
    grad_sum = lax.psum_scatter(
        combined.astype(jnp.bfloat16), "depth", scatter_dimension=1, tiled=True
    )
    return (out_final, back_final, grad_sum)


def solution(mesh):
    placed = (P("depth", "col"), P("col", ("row", "depth")), P(), P("depth", "row"), P())
    return jax.shard_map(
        shards,
        mesh=mesh,
        in_specs=placed,
        out_specs=(P("depth", "row"), P("depth", "col"), P("col", ("row", "depth"))),
        check_vma=False,
    )
```

```python
import math

import jax
import jax.numpy as jnp
from jax import lax
from jax.experimental import pallas as pl
from jax.experimental.pallas import tpu as pltpu
from jax.sharding import PartitionSpec as P

D = 8192
FW = 14336
BLOCK = 128
TOK_DEV = 1024
EX_DEV = 2
RING = 4
TILE = 256

MESH = pl.DeviceIdType.MESH
F32 = jnp.float32
BF16 = jnp.bfloat16


def kernel(
    tok_ref, w_ref, g_ref, keep_ref, pick_ref,
    out_ref, back_ref, gw_ref,
    x, xt, w, g, part, red, fin,
    fwd1, rcv1, fwd2, rcv2,
    prod, sq, bpart, brcv, bsum, blk, brecv, nrm, nrcv,
    send_sem, recv_sem, local_sem,
):
    row, col, dep = lax.axis_index("row"), lax.axis_index("col"), lax.axis_index("depth")
    y, z = lax.rem(col, RING), lax.div(col, RING)
    other = 1 - dep
    tok_rows, width = x.shape
    half = w.shape[2]
    lane_half = half // 2
    tiles = half // TILE
    crow = tok_rows // 2
    q1 = crow // RING
    q2 = q1 // RING
    qx = tok_rows // RING

    def turn(at, k):
        return lax.rem(at + (k + RING), RING)

    def device(axis, k):
        if axis == "x":
            return (turn(row, k), col, dep)
        if axis == "y":
            return (row, z * RING + turn(y, k), dep)
        if axis == "z":
            return (row, turn(z, k) * RING + y, dep)
        return (row, col, other)

    place = {"x": row, "y": y, "z": z}
    started = []
    local_started = []

    def remote(src, dst, to):
        k = len(started)
        copy = pltpu.make_async_remote_copy(
            src_ref=src, dst_ref=dst, send_sem=send_sem.at[k], recv_sem=recv_sem.at[k],
            device_id=to, device_id_type=MESH,
        )
        copy.start()
        started.append(copy)
        return copy

    def local(src, dst):
        copy = pltpu.make_async_copy(src, dst, local_sem.at[len(local_started)])
        copy.start()
        local_started.append(copy)
        return copy

    load_x = local(tok_ref, x)
    load_w = local(w_ref, w.at[dep])
    load_g = [local(g_ref.at[:, pl.ds(h * half, half)], g.at[h]) for h in range(2)]
    peers = [device(axis, k) for axis in ("y", "z", "x") for k in (1, 2, 3)] + [device("d", 1)]
    barrier = pltpu.get_barrier_semaphore()
    for peer in peers:
        pl.semaphore_signal(barrier, inc=1, device_id=peer, device_id_type=MESH)
    pl.semaphore_wait(barrier, len(peers))

    swap_w = remote(w_ref, w.at[dep], device("d", 1))

    left, right = pl.ds(0, lane_half), pl.ds(lane_half, lane_half)

    def add_into(size, dst, terms):
        def step(i, c):
            at = pl.ds(pl.multiple_of(i * 16, 16), 16)
            total = terms[0][at, :].astype(F32)
            for term in terms[1:]:
                total = total + term[at, :].astype(F32)
            dst[at, :] = total.astype(BF16)
            return c
        lax.fori_loop(0, size // 16, step, 0)

    class Reduce:
        def __init__(self, axis, size, src, fwd, rcv, dst):
            self.axis, self.size, self.fwd, self.rcv, self.dst = axis, size, fwd, rcv, dst
            me = place[axis]
            self.piece = lambda k: src.at[pl.ds(pl.multiple_of(turn(me, k) * size, size), size), :]
            self.up, self.down = device(axis, 1), device(axis, -1)

        def start(self):
            far, near, back = self.piece(2), self.piece(1), self.piece(-1)
            self.a = [
                remote(far.at[:, left], self.fwd.at[0], self.up),
                remote(far.at[:, right], self.fwd.at[1], self.down),
            ]
            self.b = [
                remote(near.at[:, right], self.rcv.at[0, :, right], self.up),
                remote(back.at[:, left], self.rcv.at[1, :, left], self.down),
            ]

        def mid(self):
            near, back = self.piece(1).at[:, left], self.piece(-1).at[:, right]
            self.a[0].wait_recv()
            add_into(self.size, near, [near, self.fwd.at[0]])
            c0 = remote(near, self.rcv.at[0, :, left], self.up)
            self.a[1].wait_recv()
            add_into(self.size, back, [back, self.fwd.at[1]])
            c1 = remote(back, self.rcv.at[1, :, right], self.down)
            self.c = [c0, c1]

        def end(self):
            for copy in self.b + self.c:
                copy.wait_recv()
            add_into(self.size, self.dst, [self.piece(0), self.rcv.at[0], self.rcv.at[1]])

    class Gather:
        def __init__(self, axis, dst):
            self.dst, me = dst, place[axis]
            self.at = lambda k: dst(turn(me, k))
            self.up, self.down = device(axis, 1), device(axis, -1)

        def start(self, src):
            own = self.at(0)
            self.ul = remote(src.at[:, left], own.at[:, left], self.up)
            self.dr = remote(src.at[:, right], own.at[:, right], self.down)
            self.ur = remote(src.at[:, right], own.at[:, right], self.up)
            self.dl = remote(src.at[:, left], own.at[:, left], self.down)

        def mid(self):
            below, above = self.at(-1).at[:, left], self.at(1).at[:, right]
            self.ul.wait_recv()
            self.f0 = remote(below, below, self.up)
            self.dr.wait_recv()
            self.f1 = remote(above, above, self.down)

        def end(self):
            for copy in (self.ur, self.dl, self.f0, self.f1):
                copy.wait_recv()

    subs = []
    for s in range(4):
        first, second = ("y", "z") if s % 2 == 0 else ("z", "y")
        base = (s % 2) * crow
        cols = pl.ds(pl.multiple_of((dep if s < 2 else other) * half, BLOCK), half)
        i1, i2 = place[first], place[second]

        def inner(i, base=base, cols=cols, i1=i1):
            return out_ref.at[pl.ds(pl.multiple_of(base + i1 * q1 + i * q2, q2), q2), cols]

        def outer(i, base=base, cols=cols):
            return out_ref.at[pl.ds(pl.multiple_of(base + i * q1, q1), q1), cols]

        subs.append(dict(
            r1=Reduce(first, q1, part.at[s], fwd1.at[s], rcv1.at[s], red.at[s]),
            r2=Reduce(second, q2, red.at[s], fwd2.at[s], rcv2.at[s], fin.at[s]),
            a1=Gather(second, inner), a2=Gather(first, outer), fin=fin.at[s],
        ))

    def r1_end(s):
        subs[s]["r1"].end()
        subs[s]["r2"].start()

    def r2_mid(s):
        subs[s]["r2"].mid()

    def r2_end(s):
        subs[s]["r2"].end()
        sub = subs[s]
        sub["a1"].start(sub["fin"])
        sub["own"] = local(sub["fin"], sub["a1"].at(0))

    def a1_mid(s):
        subs[s]["a1"].mid()

    def a1_end(s):
        sub = subs[s]
        sub["a1"].end()
        sub["own"].wait()
        sub["a2"].start(sub["a2"].at(0))

    def a2_mid(s):
        subs[s]["a2"].mid()

    def a2_end(s):
        subs[s]["a2"].end()

    def part_dot(s, mask):
        h = dep if s < 2 else other
        rows = pl.ds((s % 2) * crow, crow)

        def step(j, c):
            at = pl.ds(pl.multiple_of(j * TILE, TILE), TILE)
            if mask:
                for kb in range(width // BLOCK):
                    ks = pl.ds(kb * BLOCK, BLOCK)
                    kept = keep_ref[h, kb:kb + 1, at] > 0
                    w[h, ks, at] = jnp.where(kept, w[h, ks, at].astype(F32), 0.0).astype(BF16)
            part[s, :, at] = jnp.dot(x[rows, :], w[h, :, at], preferred_element_type=F32).astype(BF16)
            return c

        lax.fori_loop(0, tiles, step, 0)

    def make_xt():
        for i in range(tok_rows // TILE):
            at = pl.ds(i * TILE, TILE)
            flipped = jnp.transpose(x[at, :].astype(F32))
            for slot in range(EX_DEV):
                chosen = pick_ref[slot:slot + 1, at] > 0
                xt[slot, :, at] = jnp.where(chosen, flipped, 0.0).astype(BF16)

    def products(h, first, last):
        def step(j, c):
            at = pl.ds(pl.multiple_of(j * TILE, TILE), TILE)
            for slot in range(EX_DEV):
                value = jnp.dot(xt[slot], g[h, :, at], preferred_element_type=F32)
                total = sq[slot]
                for kb in range(width // BLOCK):
                    kept = keep_ref[h, kb:kb + 1, at] > 0
                    piece = jnp.where(kept, value[kb * BLOCK:(kb + 1) * BLOCK, :], 0.0)
                    prod[slot, h, pl.ds(kb * BLOCK, BLOCK), at] = piece
                    total = total + jnp.sum((piece * piece).reshape(BLOCK // 8, 8, TILE), axis=0)
                sq[slot] = total
            return c

        lax.fori_loop(first, last, step, 0)

    def back_dot():
        def step(i, c):
            rows = pl.ds(pl.multiple_of(i * TILE, TILE), TILE)
            total = None
            for h in range(2):
                term = lax.dot_general(
                    g[h, rows, :], w[h], (((1,), (1,)), ((), ())), preferred_element_type=F32
                )
                total = term if total is None else total + term
            bpart[rows, :] = total.astype(BF16)
            return c

        lax.fori_loop(0, tok_rows // TILE, step, 0)

    quarter = lambda ref, i: ref.at[pl.ds(pl.multiple_of(i * qx, qx), qx), :]
    state = {}

    def back_send():
        state["b"] = [remote(quarter(bpart, turn(row, k)), brcv.at[k - 1], device("x", k)) for k in (2, 1, 3)]

    def back_sum():
        for copy in state["b"]:
            copy.wait_recv()
        add_into(qx, bsum, [quarter(bpart, row), brcv.at[0], brcv.at[1], brcv.at[2]])
        state["bg"] = [remote(bsum, quarter(back_ref, row), device("x", k)) for k in (2, 1, 3)]
        state["bl"] = local(bsum, quarter(back_ref, row))

    def norm_first():
        rows = lax.broadcasted_iota(jnp.int32, (8, TILE), 0)
        first, second = jnp.sum(sq[0]), jnp.sum(sq[1])
        nrm[0] = jnp.where(rows == 0, first, jnp.where(rows == 1, second, 0.0))

    def norm_send(stage):
        axis = "xyz"[stage]
        state["n"] = [remote(nrm.at[stage], nrcv.at[stage, k - 1], device(axis, k)) for k in (1, 2, 3)]

    def norm_sum(stage):
        for copy in state["n"]:
            copy.wait_recv()
        nrm[stage + 1] = nrm[stage] + nrcv[stage, 0] + nrcv[stage, 1] + nrcv[stage, 2]

    def block_sums():
        bound = F32(0.5 * math.sqrt(D * FW * TOK_DEV))
        factors = bound / jnp.maximum(jnp.sqrt(nrm[3]), bound)
        f0, f1 = factors[0:1, :], factors[1:2, :]

        for h in range(2):
            def step(j, c, h=h):
                at = pl.ds(pl.multiple_of(j * TILE, TILE), TILE)
                total = f0 * prod[0, h, :, at] + f1 * prod[1, h, :, at]
                blk[h, :, at] = (total * 0.25).astype(BF16)
                return c
            lax.fori_loop(0, tiles, step, 0)
        state["w"] = remote(blk.at[other], brecv, device("d", 1))

    def weight_sum():
        state["w"].wait_recv()
        add_into(width, brecv, [blk.at[dep], brecv])
        state["wl"] = local(brecv, gw_ref)

    load_x.wait()
    load_w.wait()
    part_dot(0, True)
    subs[0]["r1"].start()
    part_dot(1, False)
    subs[1]["r1"].start()
    swap_w.wait_recv()
    part_dot(2, True)
    part_dot(3, False)
    subs[0]["r1"].mid()
    subs[2]["r1"].start()
    subs[1]["r1"].mid()
    subs[3]["r1"].start()
    make_xt()
    for slot in range(EX_DEV):
        sq[slot] = jnp.zeros((8, TILE), F32)
    for copy in load_g:
        copy.wait()
    products(0, 0, 5)
    r1_end(0)
    r1_end(1)
    products(0, 5, tiles)
    products(1, 0, 3)
    subs[2]["r1"].mid()
    subs[3]["r1"].mid()
    r2_mid(0)
    r2_mid(1)
    products(1, 3, tiles)
    norm_first()
    norm_send(0)
    r2_end(0)
    r2_end(1)
    back_dot()
    back_send()
    norm_sum(0)
    norm_send(1)
    a1_mid(0)
    a1_mid(1)
    r1_end(2)
    r1_end(3)
    a1_end(0)
    a1_end(1)
    norm_sum(1)
    norm_send(2)
    r2_mid(2)
    r2_mid(3)
    back_sum()
    norm_sum(2)
    block_sums()
    r2_end(2)
    r2_end(3)
    a2_mid(0)
    a2_mid(1)
    a1_mid(2)
    a1_mid(3)
    weight_sum()
    a1_end(2)
    a1_end(3)
    a2_end(0)
    a2_end(1)
    a2_mid(2)
    a2_mid(3)
    for copy in state["bg"]:
        copy.wait_recv()
    a2_end(2)
    a2_end(3)
    for copy in started:
        copy.wait_send()
    state["bl"].wait()
    state["wl"].wait()


def shards(tokens, weight, block_mask, cotangent, example_ids):
    tok_rows, width = tokens.shape
    half = weight.shape[1]
    hidden = cotangent.shape[1]
    col_at, row_at, depth_at = lax.axis_index("col"), lax.axis_index("row"), lax.axis_index("depth")
    deep, wide = width // BLOCK, hidden // BLOCK
    tile_mask = lax.dynamic_slice(block_mask, (col_at * deep, row_at * wide), (deep, wide))
    keep = jnp.repeat((tile_mask > 0).astype(F32), BLOCK, axis=1).reshape(deep, 2, half).transpose(1, 0, 2)
    ids_here = lax.dynamic_slice_in_dim(example_ids, depth_at * tok_rows, tok_rows)
    pick = (ids_here[None, :] == depth_at * EX_DEV + jnp.arange(EX_DEV, dtype=jnp.int32)[:, None]).astype(F32)
    crow = tok_rows // 2
    q1, q2, qx = crow // RING, crow // RING // RING, tok_rows // RING
    vmem = pl.BlockSpec(memory_space=pltpu.VMEM)
    anywhere = pl.BlockSpec(memory_space=pl.ANY)
    copies = 1 + 4 * 24 + 6 + 9 + 1
    return pl.pallas_call(
        kernel,
        out_shape=(
            jax.ShapeDtypeStruct((tok_rows, hidden), BF16),
            jax.ShapeDtypeStruct((tok_rows, width), BF16),
            jax.ShapeDtypeStruct((width, half), BF16),
        ),
        in_specs=[anywhere, anywhere, anywhere, vmem, vmem],
        out_specs=(anywhere, anywhere, anywhere),
        scratch_shapes=[
            pltpu.VMEM((tok_rows, width), BF16),
            pltpu.VMEM((EX_DEV, width, tok_rows), BF16),
            pltpu.VMEM((2, width, half), BF16),
            pltpu.VMEM((2, tok_rows, half), BF16),
            pltpu.VMEM((4, crow, half), BF16),
            pltpu.VMEM((4, q1, half), BF16),
            pltpu.VMEM((4, q2, half), BF16),
            pltpu.VMEM((4, 2, q1, half // 2), BF16),
            pltpu.VMEM((4, 2, q1, half), BF16),
            pltpu.VMEM((4, 2, q2, half // 2), BF16),
            pltpu.VMEM((4, 2, q2, half), BF16),
            pltpu.VMEM((EX_DEV, 2, width, half), F32),
            pltpu.VMEM((EX_DEV, 8, TILE), F32),
            pltpu.VMEM((tok_rows, width), BF16),
            pltpu.VMEM((3, qx, width), BF16),
            pltpu.VMEM((qx, width), BF16),
            pltpu.VMEM((2, width, half), BF16),
            pltpu.VMEM((width, half), BF16),
            pltpu.VMEM((4, 8, TILE), F32),
            pltpu.VMEM((3, 3, 8, TILE), F32),
            pltpu.SemaphoreType.DMA((copies,)),
            pltpu.SemaphoreType.DMA((copies,)),
            pltpu.SemaphoreType.DMA((10,)),
        ],
        compiler_params=pltpu.CompilerParams(
            collective_id=0, has_side_effects=True, vmem_limit_bytes=67_000_000
        ),
        name="whole_layer",
    )(tokens, weight, cotangent, keep, pick)


def solution(mesh):
    placed = (P("depth", "col"), P("col", ("row", "depth")), P(), P("depth", "row"), P())
    return jax.shard_map(
        shards,
        mesh=mesh,
        in_specs=placed,
        out_specs=(P("depth", "row"), P("depth", "col"), P("col", ("row", "depth"))),
        check_vma=False,
    )
```

```python
import math

import jax
import jax.numpy as jnp
from jax import lax
from jax.experimental import pallas as pl
from jax.experimental.pallas import tpu as pltpu
from jax.sharding import PartitionSpec as P

D = 8192
FW = 14336
BLOCK = 128
TOK_DEV = 1024
EX_DEV = 2
RING = 4
TILE = 256

MESH = pl.DeviceIdType.MESH
F32 = jnp.float32
BF16 = jnp.bfloat16


def kernel(
    tok_ref, w_ref, g_ref, mask_ref, ids_ref,
    out_ref, back_ref, gw_ref,
    x, xt, w, g, part, red, fin,
    fwd1, rcv1, fwd2, rcv2,
    prod, sq, bpart, brcv, bsum, blk, brecv, nrm, nrcv, keep_ref,
    send_sem, recv_sem, local_sem,
):
    row, col, dep = lax.axis_index("row"), lax.axis_index("col"), lax.axis_index("depth")
    y, z = lax.rem(col, RING), lax.div(col, RING)
    other = 1 - dep
    tok_rows, width = x.shape
    half = w.shape[2]
    lane_half = half // 2
    tiles = half // TILE
    crow = tok_rows // 2
    q1 = crow // RING
    q2 = q1 // RING
    qx = tok_rows // RING

    def turn(at, k):
        return lax.rem(at + (k + RING), RING)

    def device(axis, k):
        if axis == "x":
            return (turn(row, k), col, dep)
        if axis == "y":
            return (row, z * RING + turn(y, k), dep)
        if axis == "z":
            return (row, turn(z, k) * RING + y, dep)
        return (row, col, other)

    place = {"x": row, "y": y, "z": z}
    started = []
    local_started = []

    def remote(src, dst, to):
        k = len(started)
        copy = pltpu.make_async_remote_copy(
            src_ref=src, dst_ref=dst, send_sem=send_sem.at[k], recv_sem=recv_sem.at[k],
            device_id=to, device_id_type=MESH,
        )
        copy.start()
        started.append(copy)
        return copy

    def local(src, dst):
        copy = pltpu.make_async_copy(src, dst, local_sem.at[len(local_started)])
        copy.start()
        local_started.append(copy)
        return copy

    load_x = local(tok_ref, x)
    load_w = local(w_ref, w.at[dep])
    load_g = [local(g_ref.at[:, pl.ds(h * half, half)], g.at[h]) for h in range(2)]
    peers = [device(axis, k) for axis in ("y", "z", "x") for k in (1, 2, 3)] + [device("d", 1)]
    barrier = pltpu.get_barrier_semaphore()
    for peer in peers:
        pl.semaphore_signal(barrier, inc=1, device_id=peer, device_id_type=MESH)
    left, right = pl.ds(0, lane_half), pl.ds(lane_half, lane_half)

    def add_into(size, dst, terms):
        def step(i, c):
            at = pl.ds(pl.multiple_of(i * 16, 16), 16)
            total = terms[0][at, :].astype(F32)
            for term in terms[1:]:
                total = total + term[at, :].astype(F32)
            dst[at, :] = total.astype(BF16)
            return c
        lax.fori_loop(0, size // 16, step, 0)

    class Reduce:
        def __init__(self, axis, size, src, fwd, rcv, dst):
            self.axis, self.size, self.fwd, self.rcv, self.dst = axis, size, fwd, rcv, dst
            me = place[axis]
            self.piece = lambda k: src.at[pl.ds(pl.multiple_of(turn(me, k) * size, size), size), :]
            self.up, self.down = device(axis, 1), device(axis, -1)

        def start(self):
            far, near, back = self.piece(2), self.piece(1), self.piece(-1)
            self.a = [
                remote(far.at[:, left], self.fwd.at[0], self.up),
                remote(far.at[:, right], self.fwd.at[1], self.down),
            ]
            self.b = [
                remote(near.at[:, right], self.rcv.at[0, :, right], self.up),
                remote(back.at[:, left], self.rcv.at[1, :, left], self.down),
            ]

        def mid(self):
            near, back = self.piece(1).at[:, left], self.piece(-1).at[:, right]
            self.a[0].wait_recv()
            add_into(self.size, near, [near, self.fwd.at[0]])
            c0 = remote(near, self.rcv.at[0, :, left], self.up)
            self.a[1].wait_recv()
            add_into(self.size, back, [back, self.fwd.at[1]])
            c1 = remote(back, self.rcv.at[1, :, right], self.down)
            self.c = [c0, c1]

        def end(self):
            for copy in self.b + self.c:
                copy.wait_recv()
            add_into(self.size, self.dst, [self.piece(0), self.rcv.at[0], self.rcv.at[1]])

    class Gather:
        def __init__(self, axis, dst):
            self.dst, me = dst, place[axis]
            self.at = lambda k: dst(turn(me, k))
            self.up, self.down = device(axis, 1), device(axis, -1)

        def start(self, src):
            own = self.at(0)
            self.ul = remote(src.at[:, left], own.at[:, left], self.up)
            self.dr = remote(src.at[:, right], own.at[:, right], self.down)
            self.ur = remote(src.at[:, right], own.at[:, right], self.up)
            self.dl = remote(src.at[:, left], own.at[:, left], self.down)

        def mid(self):
            below, above = self.at(-1).at[:, left], self.at(1).at[:, right]
            self.ul.wait_recv()
            self.f0 = remote(below, below, self.up)
            self.dr.wait_recv()
            self.f1 = remote(above, above, self.down)

        def end(self):
            for copy in (self.ur, self.dl, self.f0, self.f1):
                copy.wait_recv()

    subs = []
    for s in range(4):
        first, second = ("y", "z") if s % 2 == 0 else ("z", "y")
        base = (s % 2) * crow
        cols = pl.ds(pl.multiple_of((dep if s < 2 else other) * half, BLOCK), half)
        i1, i2 = place[first], place[second]

        def inner(i, base=base, cols=cols, i1=i1):
            return out_ref.at[pl.ds(pl.multiple_of(base + i1 * q1 + i * q2, q2), q2), cols]

        def outer(i, base=base, cols=cols):
            return out_ref.at[pl.ds(pl.multiple_of(base + i * q1, q1), q1), cols]

        subs.append(dict(
            r1=Reduce(first, q1, part.at[s], fwd1.at[s], rcv1.at[s], red.at[s]),
            r2=Reduce(second, q2, red.at[s], fwd2.at[s], rcv2.at[s], fin.at[s]),
            a1=Gather(second, inner), a2=Gather(first, outer), fin=fin.at[s],
        ))

    def r1_end(s):
        subs[s]["r1"].end()
        subs[s]["r2"].start()

    def r2_mid(s):
        subs[s]["r2"].mid()

    def r2_end(s):
        subs[s]["r2"].end()
        sub = subs[s]
        sub["a1"].start(sub["fin"])
        sub["own"] = local(sub["fin"], sub["a1"].at(0))

    def a1_mid(s):
        subs[s]["a1"].mid()

    def a1_end(s):
        sub = subs[s]
        sub["a1"].end()
        sub["own"].wait()
        sub["a2"].start(sub["a2"].at(0))

    def a2_mid(s):
        subs[s]["a2"].mid()

    def a2_end(s):
        subs[s]["a2"].end()

    def expand_mask():
        blocks_in, blocks_out = mask_ref.shape
        deep, wide = width // BLOCK, 2 * half // BLOCK
        kept = (mask_ref[...] > 0).astype(F32).astype(BF16)
        here = lax.broadcasted_iota(jnp.int32, (8, blocks_in), 0)
        there = lax.broadcasted_iota(jnp.int32, (8, blocks_in), 1)
        pick_rows = ((there == here + col * deep) & (here < deep)).astype(F32).astype(BF16)
        rows = jnp.dot(pick_rows, kept, preferred_element_type=F32).astype(BF16)
        block = lax.broadcasted_iota(jnp.int32, (blocks_out, half), 0)
        lane = lax.broadcasted_iota(jnp.int32, (blocks_out, half), 1)
        for h in range(2):
            spread = (block == row * wide + h * (half // BLOCK) + lane // BLOCK).astype(F32).astype(BF16)
            keep_ref[h] = jnp.dot(rows, spread, preferred_element_type=F32)

    def part_dot(s, mask):
        h = dep if s < 2 else other
        rows = pl.ds((s % 2) * crow, crow)

        def step(j, c):
            at = pl.ds(pl.multiple_of(j * TILE, TILE), TILE)
            if mask:
                for kb in range(width // BLOCK):
                    ks = pl.ds(kb * BLOCK, BLOCK)
                    kept = keep_ref[h, kb:kb + 1, at] > 0
                    w[h, ks, at] = jnp.where(kept, w[h, ks, at].astype(F32), 0.0).astype(BF16)
            part[s, :, at] = jnp.dot(x[rows, :], w[h, :, at], preferred_element_type=F32).astype(BF16)
            return c

        lax.fori_loop(0, tiles, step, 0)

    def make_xt():
        first_id = (ids_ref[...] == dep * EX_DEV).astype(F32)
        run = jnp.sum(jnp.sum(first_id, axis=0, keepdims=True), axis=1, keepdims=True)
        token = lax.broadcasted_iota(jnp.int32, (1, TILE), 1).astype(F32)
        for i in range(tok_rows // TILE):
            at = pl.ds(i * TILE, TILE)
            flipped = jnp.transpose(x[at, :].astype(F32))
            for slot in range(EX_DEV):
                chosen = (token + i * TILE < run) if slot == 0 else (token + i * TILE >= run)
                xt[slot, :, at] = jnp.where(chosen, flipped, 0.0).astype(BF16)

    def products(h, first, last):
        def step(j, c):
            at = pl.ds(pl.multiple_of(j * TILE, TILE), TILE)
            for slot in range(EX_DEV):
                value = jnp.dot(xt[slot], g[h, :, at], preferred_element_type=F32)
                total = sq[slot]
                for kb in range(width // BLOCK):
                    kept = keep_ref[h, kb:kb + 1, at] > 0
                    piece = jnp.where(kept, value[kb * BLOCK:(kb + 1) * BLOCK, :], 0.0)
                    prod[slot, h, pl.ds(kb * BLOCK, BLOCK), at] = piece
                    total = total + jnp.sum((piece * piece).reshape(BLOCK // 8, 8, TILE), axis=0)
                sq[slot] = total
            return c

        lax.fori_loop(first, last, step, 0)

    def back_dot():
        def step(i, c):
            rows = pl.ds(pl.multiple_of(i * TILE, TILE), TILE)
            total = None
            for h in range(2):
                term = lax.dot_general(
                    g[h, rows, :], w[h], (((1,), (1,)), ((), ())), preferred_element_type=F32
                )
                total = term if total is None else total + term
            bpart[rows, :] = total.astype(BF16)
            return c

        lax.fori_loop(0, tok_rows // TILE, step, 0)

    quarter = lambda ref, i: ref.at[pl.ds(pl.multiple_of(i * qx, qx), qx), :]
    state = {}

    def back_send():
        state["b"] = [remote(quarter(bpart, turn(row, k)), brcv.at[k - 1], device("x", k)) for k in (2, 1, 3)]

    def back_sum():
        for copy in state["b"]:
            copy.wait_recv()
        add_into(qx, bsum, [quarter(bpart, row), brcv.at[0], brcv.at[1], brcv.at[2]])
        state["bg"] = [remote(bsum, quarter(back_ref, row), device("x", k)) for k in (2, 1, 3)]
        state["bl"] = local(bsum, quarter(back_ref, row))

    def norm_first():
        rows = lax.broadcasted_iota(jnp.int32, (8, TILE), 0)
        first, second = jnp.sum(sq[0]), jnp.sum(sq[1])
        nrm[0] = jnp.where(rows == 0, first, jnp.where(rows == 1, second, 0.0))

    def norm_send(stage):
        axis = "xyz"[stage]
        state["n"] = [remote(nrm.at[stage], nrcv.at[stage, k - 1], device(axis, k)) for k in (1, 2, 3)]

    def norm_sum(stage):
        for copy in state["n"]:
            copy.wait_recv()
        nrm[stage + 1] = nrm[stage] + nrcv[stage, 0] + nrcv[stage, 1] + nrcv[stage, 2]

    def block_sums():
        bound = F32(0.5 * math.sqrt(D * FW * TOK_DEV))
        factors = bound / jnp.maximum(jnp.sqrt(nrm[3]), bound)
        f0, f1 = factors[0:1, :], factors[1:2, :]

        for h in range(2):
            def step(j, c, h=h):
                at = pl.ds(pl.multiple_of(j * TILE, TILE), TILE)
                total = f0 * prod[0, h, :, at] + f1 * prod[1, h, :, at]
                blk[h, :, at] = (total * 0.25).astype(BF16)
                return c
            lax.fori_loop(0, tiles, step, 0)
        state["w"] = remote(blk.at[other], brecv, device("d", 1))

    def weight_sum():
        state["w"].wait_recv()
        add_into(width, brecv, [blk.at[dep], brecv])
        state["wl"] = local(brecv, gw_ref)

    expand_mask()
    load_x.wait()
    load_w.wait()
    part_dot(0, True)
    pl.semaphore_wait(barrier, len(peers))
    swap_w = remote(w_ref, w.at[dep], device("d", 1))
    subs[0]["r1"].start()
    part_dot(1, False)
    subs[1]["r1"].start()
    swap_w.wait_recv()
    part_dot(2, True)
    part_dot(3, False)
    subs[0]["r1"].mid()
    subs[2]["r1"].start()
    subs[1]["r1"].mid()
    subs[3]["r1"].start()
    make_xt()
    for slot in range(EX_DEV):
        sq[slot] = jnp.zeros((8, TILE), F32)
    for copy in load_g:
        copy.wait()
    products(0, 0, 5)
    r1_end(0)
    r1_end(1)
    products(0, 5, tiles)
    products(1, 0, 3)
    subs[2]["r1"].mid()
    subs[3]["r1"].mid()
    r2_mid(0)
    r2_mid(1)
    products(1, 3, tiles)
    norm_first()
    norm_send(0)
    r2_end(0)
    r2_end(1)
    back_dot()
    back_send()
    norm_sum(0)
    norm_send(1)
    a1_mid(0)
    a1_mid(1)
    r1_end(2)
    r1_end(3)
    a1_end(0)
    a1_end(1)
    norm_sum(1)
    norm_send(2)
    r2_mid(2)
    r2_mid(3)
    back_sum()
    norm_sum(2)
    block_sums()
    r2_end(2)
    r2_end(3)
    a2_mid(0)
    a2_mid(1)
    a1_mid(2)
    a1_mid(3)
    weight_sum()
    a1_end(2)
    a1_end(3)
    a2_end(0)
    a2_end(1)
    a2_mid(2)
    a2_mid(3)
    for copy in state["bg"]:
        copy.wait_recv()
    a2_end(2)
    a2_end(3)
    for copy in started:
        copy.wait_send()
    state["bl"].wait()
    state["wl"].wait()


def shards(tokens, weight, block_mask, cotangent, example_ids):
    tok_rows, width = tokens.shape
    half = weight.shape[1]
    hidden = cotangent.shape[1]
    ids = example_ids.reshape(-1, BLOCK)
    crow = tok_rows // 2
    q1, q2, qx = crow // RING, crow // RING // RING, tok_rows // RING
    vmem = pl.BlockSpec(memory_space=pltpu.VMEM)
    anywhere = pl.BlockSpec(memory_space=pl.ANY)
    copies = 1 + 4 * 24 + 6 + 9 + 1
    return pl.pallas_call(
        kernel,
        out_shape=(
            pltpu.VMEM((tok_rows, hidden), BF16),
            pltpu.VMEM((tok_rows, width), BF16),
            pltpu.VMEM((width, half), BF16),
        ),
        in_specs=[anywhere, anywhere, anywhere, vmem, vmem],
        out_specs=(vmem, vmem, vmem),
        scratch_shapes=[
            pltpu.VMEM((tok_rows, width), BF16),
            pltpu.VMEM((EX_DEV, width, tok_rows), BF16),
            pltpu.VMEM((2, width, half), BF16),
            pltpu.VMEM((2, tok_rows, half), BF16),
            pltpu.VMEM((4, crow, half), BF16),
            pltpu.VMEM((4, q1, half), BF16),
            pltpu.VMEM((4, q2, half), BF16),
            pltpu.VMEM((4, 2, q1, half // 2), BF16),
            pltpu.VMEM((4, 2, q1, half), BF16),
            pltpu.VMEM((4, 2, q2, half // 2), BF16),
            pltpu.VMEM((4, 2, q2, half), BF16),
            pltpu.VMEM((EX_DEV, 2, width, half), F32),
            pltpu.VMEM((EX_DEV, 8, TILE), F32),
            pltpu.VMEM((tok_rows, width), BF16),
            pltpu.VMEM((3, qx, width), BF16),
            pltpu.VMEM((qx, width), BF16),
            pltpu.VMEM((2, width, half), BF16),
            pltpu.VMEM((width, half), BF16),
            pltpu.VMEM((4, 8, TILE), F32),
            pltpu.VMEM((3, 3, 8, TILE), F32),
            pltpu.VMEM((2, 8, half), F32),
            pltpu.SemaphoreType.DMA((copies,)),
            pltpu.SemaphoreType.DMA((copies,)),
            pltpu.SemaphoreType.DMA((10,)),
        ],
        compiler_params=pltpu.CompilerParams(
            collective_id=0, has_side_effects=True, vmem_limit_bytes=56_000_000
        ),
        name="whole_layer",
    )(tokens, weight, cotangent, block_mask, ids)


def solution(mesh):
    placed = (P("depth", "col"), P("col", ("row", "depth")), P(), P("depth", "row"), P())
    return jax.shard_map(
        shards,
        mesh=mesh,
        in_specs=placed,
        out_specs=(P("depth", "row"), P("depth", "col"), P("col", ("row", "depth"))),
        check_vma=False,
    )
```
